32 devices in a mesh: dp: 1, center: 32 (over z, y, x, core).
Axes of the slice: x: 2, y: 2, z: 4, core: 2. Of those that a mesh axis runs over, the one named last changes fastest.
Arguments:
- embeddings: bfloat16 [1024, 2048], P('dp', 'center'), may hold values from -6 to 6
- first_weight: bfloat16 [2048, 2048], P(None, 'center'), may hold values from -0.125 to 0.125
- first_bias: float32 [2048], P('center'), may hold values from -3 to 3
- second_weight: bfloat16 [2048, 512], P('center'), may hold values from -0.1875 to 0.1875
- centers: bfloat16 [65536, 512], P('center'), may hold values from -4 to 4
- coefficients: bfloat16 [65536, 100], P('center'), may hold values from -12 to 12
- cotangent: bfloat16 [1024, 100], P('dp'), may hold values from -18 to 18
Outputs:
- predictions: float32 [1024, 100], P(('dp', 'center'))
- grad_first: float32 [2048, 2048], P('dp', 'center')
- grad_bias: float32 [2048], P('center')
- grad_second: float32 [2048, 512], P('center', 'dp')
- grad_centers: float32 [65536, 512], P('center', 'dp')
- grad_coefs: float32 [65536, 100], P('center')
The draws below stay inside these ranges and needn't reach their ends.
All inputs are finite; a program needn't handle non-finite values.
Results may differ from the reference program's by a relative error of at most 0.028.
Values may be sent and summed in bfloat16 or wider, within the bound.
No kernel may reach another device: no remote copies, remote signals or barrier semaphores. Data moves between devices by JAX's collectives and lax.ppermute only.
A program may use at most 64 MiB of HBM per device.

```python
import jax
import jax.numpy as jnp
from jax import lax

DIN = 2048
HID = 2048
FEAT = 512
OUT = 100
CDEV = 2048
BATCH = 1024
M = 65536


def block_scale(key, shape, pieces, smallest, largest):
    def one(dim, shards_of):
        heights = jax.random.uniform(jax.random.fold_in(jax.random.fold_in(key, 6), dim), (shards_of,), jnp.float32, smallest / len(pieces), largest / len(pieces))
        return jnp.repeat(jnp.exp(heights), shape[dim] // shards_of).reshape((-1,) + (1,) * (len(shape) - dim - 1))

    gain = one(*pieces[0])
    for cut in pieces[1:]:
        gain = gain * one(*cut)
    return gain


def normal_values(own_key, dims, deviation, reach, split=(), held_as=jnp.bfloat16):
    entries = deviation * jax.random.normal(own_key, dims, jnp.float32)
    if split:
        entries = entries * block_scale(own_key, dims, split, -0.22, 0.18)
    return jnp.clip(entries, -reach, reach).astype(held_as)


def setup_inputs(seed: int = 0) -> dict:
    splits = jax.random.split(jax.random.key(seed), 8)
    embeddings = normal_values(splits[0], (BATCH, DIN), 1.0, 6.0, ((1, 32),))
    first_weight = normal_values(splits[1], (DIN, HID), DIN ** -0.5, 0.125, ((1, 32),))
    first_bias = normal_values(splits[2], (HID,), 0.5, 3.0, ((0, 32),), jnp.float32)
    second_weight = normal_values(splits[3], (HID, FEAT), (HID // 2) ** -0.5, 0.1875, ((0, 32),))
    centers = normal_values(splits[4], (M, FEAT), 0.6, 4.0, ((0, 32),))
    coefficients = normal_values(splits[5], (M, OUT), 2.0, 12.0, ((0, 32),))
    cotangent = normal_values(splits[6], (BATCH, OUT), 3.0, 18.0)
    return {"embeddings": embeddings, "first_weight": first_weight, "first_bias": first_bias, "second_weight": second_weight, "centers": centers, "coefficients": coefficients, "cotangent": cotangent}


def reference(embeddings, first_weight, first_bias, second_weight, centers, coefficients, cotangent):
    preact = jnp.dot(embeddings, first_weight, preferred_element_type=jnp.float32) + first_bias
    hidden = jax.nn.gelu(preact).astype(jnp.bfloat16)
    feature_sum = jnp.dot(hidden, second_weight, preferred_element_type=jnp.float32)
    squashed = jnp.tanh(feature_sum)
    features = squashed.astype(jnp.bfloat16)
    feat_wide = features.astype(jnp.float32)
    feat_norms = lax.optimization_barrier(jnp.sum(feat_wide * feat_wide, axis=1))
    factor = 16.0 / FEAT
    block_count = M // CDEV
    center_blocks = centers.reshape(block_count, CDEV, FEAT)
    coef_blocks = coefficients.reshape(block_count, CDEV, OUT)

    def visit(carry, block):
        pred_acc, grad_acc = carry
        center_block, coef_block = block
        center_wide = center_block.astype(jnp.float32)
        center_norms = lax.optimization_barrier(jnp.sum(center_wide * center_wide, axis=1))
        inner_prods = jnp.dot(features, center_block.T, preferred_element_type=jnp.float32)
        sq_dist = feat_norms[:, None] + center_norms[None, :] - 2.0 * inner_prods
        kernel = jnp.exp(-8.0 * sq_dist / FEAT).astype(jnp.bfloat16)
        pred_acc = pred_acc + jnp.dot(kernel, coef_block, preferred_element_type=jnp.float32)
        kernel_grad = jnp.dot(cotangent, coef_block.T, preferred_element_type=jnp.float32)
        weighted = kernel_grad * kernel.astype(jnp.float32)
        weighted_low = weighted.astype(jnp.bfloat16)
        grad_acc = grad_acc - factor * (lax.optimization_barrier(jnp.sum(weighted, axis=1))[:, None] * feat_wide - jnp.dot(weighted_low, center_block, preferred_element_type=jnp.float32))
        center_grad = -factor * (lax.optimization_barrier(jnp.sum(weighted, axis=0))[:, None] * center_wide - jnp.dot(weighted_low.T, features, preferred_element_type=jnp.float32))
        coef_grad = jnp.dot(kernel.T, cotangent, preferred_element_type=jnp.float32)
        return ((pred_acc, grad_acc), (center_grad, coef_grad))
    start_carry = (jnp.zeros((BATCH, OUT), jnp.float32), jnp.zeros((BATCH, FEAT), jnp.float32))
    (predictions, feature_grad), (center_grads, coef_grads) = lax.scan(visit, start_carry, (center_blocks, coef_blocks))
    grad_centers = center_grads.reshape(M, FEAT)
    grad_coefs = coef_grads.reshape(M, OUT)
    phi_grad = (feature_grad * (1.0 - squashed * squashed)).astype(jnp.bfloat16)
    grad_second = jnp.dot(hidden.T, phi_grad, preferred_element_type=jnp.float32)
    hidden_grad = jnp.dot(phi_grad, second_weight.T, preferred_element_type=jnp.float32)
    unused, pullback = jax.vjp(jax.nn.gelu, preact)
    preact_grad = pullback(hidden_grad)[0]
    grad_bias = lax.optimization_barrier(jnp.sum(preact_grad, axis=0))
    preact_low = preact_grad.astype(jnp.bfloat16)
    grad_first = jnp.dot(embeddings.T, preact_low, preferred_element_type=jnp.float32)
    return (predictions, grad_first, grad_bias, grad_second, grad_centers, grad_coefs)
```

```python
import jax
import jax.numpy as jnp
from jax import lax
from jax.sharding import PartitionSpec as P

BF = jnp.bfloat16
F32 = jnp.float32
CORE, X, Y, Z = 1, 2, 4, 8


def pick(bit, zero, one):
    return jnp.where(bit == 1, one, zero)


def ordered(bit, own, other, axis):
    return jnp.concatenate([pick(bit, own, other), pick(bit, other, own)], axis=axis)


def make_body(count, groups):
    deep = count // Z

    def swap(value, bit):
        return lax.ppermute(value, "center", [(i, i ^ bit) for i in range(count)])

    def owner(i):
        block = (i & 1) * 4 + ((i >> 2) & 1) * 2 + ((i >> 1) & 1)
        return deep * block + i // Z

    def body(embeddings, first_weight, first_bias, second_weight, centers, coefficients, cotangent):
        feat_width = centers.shape[1]
        factor = 16.0 / feat_width
        rows = embeddings.shape[0]
        blk = rows // 8
        place = lax.axis_index("center")
        cbit, xbit, ybit, depth = place & 1, (place >> 1) & 1, (place >> 2) & 1, place // Z
        z_bits = [Z << k for k in range(deep.bit_length() - 1)]

        cols = embeddings.shape[1]
        local = embeddings.T
        part = [
            [[local[:, (4 * c + 2 * y + x) * blk:][:, :blk] for x in range(2)] for y in range(2)]
            for c in range(2)
        ]
        cy = [(c, y) for c in range(2) for y in range(2)]
        keep = jnp.concatenate([pick(xbit, part[c][y][0], part[c][y][1]) for c, y in cy], axis=1)
        send = jnp.concatenate([pick(xbit, part[c][y][1], part[c][y][0]) for c, y in cy], axis=1)
        block = ordered(xbit, keep, swap(send, X), 0)
        halves = [[block[:, (2 * c + y) * blk:][:, :blk] for y in range(2)] for c in range(2)]
        keep = jnp.concatenate([pick(ybit, halves[c][0], halves[c][1]) for c in range(2)], axis=1)
        send = jnp.concatenate([pick(ybit, halves[c][1], halves[c][0]) for c in range(2)], axis=1)
        block = ordered(ybit, keep, swap(send, Y), 0)
        for k, bit in enumerate(z_bits):
            block = ordered((depth >> k) & 1, block, swap(block, bit), 0)
        other = swap(block, CORE)
        shape = (4 * deep, 1, cols, 2 * blk)
        emb = ordered(cbit, block.reshape(shape), other.reshape(shape), 1)
        emb = emb.reshape(count * cols, 2 * blk)

        hid = first_weight.shape[1]
        high = first_bias.astype(BF)
        low = (first_bias - high.astype(F32)).astype(BF)
        bias_cols = jnp.pad(jnp.stack([high, low], axis=1), ((0, 0), (0, 126)))
        weights = jnp.concatenate([first_weight.T, second_weight, bias_cols], axis=1)
        weights = jnp.concatenate([weights, swap(weights, X)], axis=0)
        weights = jnp.concatenate([weights, swap(weights, Y)], axis=0)
        din = first_weight.shape[0]
        w_first = weights[:, :din]
        w_second = weights[:, din:din + feat_width]
        bias = weights[:, din + feat_width:][:, :2].astype(F32).sum(axis=1, keepdims=True)

        preact = jnp.dot(w_first, emb, preferred_element_type=F32) + bias
        hidden = jax.nn.gelu(preact).astype(BF)
        part_sum = jnp.einsum("hr,hf->rf", hidden, w_second, preferred_element_type=F32)
        mine = pick(cbit, part_sum[:blk], part_sum[blk:])
        theirs = pick(cbit, part_sum[blk:], part_sum[:blk])
        total = mine + swap(theirs, CORE)

        def deep_sum(value):
            for bit in z_bits:
                low_value = value.astype(BF)
                value = low_value.astype(F32) + swap(low_value, bit).astype(F32)
            return value

        feature_sum = deep_sum(total)
        squashed = jnp.tanh(feature_sum)
        features = squashed.astype(BF)
        for bit in (Y, X, CORE):
            features = jnp.concatenate([features, swap(features, bit)], axis=0)

        cot = cotangent.T
        half, quarter = rows // 2, rows // 4
        cot = pick(cbit, cot, jnp.concatenate([cot[:, half:], cot[:, :half]], axis=1))
        pieces = []
        for c in range(2):
            quad = [cot[:, c * half + i * blk:][:, :blk] for i in range(4)]
            for x in range(2):
                for y in range(2):
                    near = pick(xbit, quad[2 * y + x], quad[2 * y + 1 - x])
                    far = pick(xbit, quad[2 * (1 - y) + x], quad[2 * (1 - y) + 1 - x])
                    pieces.append(pick(ybit, near, far))
        cot = jnp.concatenate(pieces, axis=1)

        feat_wide = features.astype(F32)
        center_wide = centers.astype(F32)
        feat_norms = jnp.sum(feat_wide * feat_wide, axis=1)
        center_norms = jnp.sum(center_wide * center_wide, axis=1)
        inner_prods = jnp.einsum("tf,cf->tc", features, centers, preferred_element_type=F32)
        sq_dist = feat_norms[:, None] + center_norms[None, :] - 2.0 * inner_prods
        kernel = jnp.exp(-8.0 * sq_dist / feat_width).astype(BF)
        pred_part = jnp.dot(kernel, coefficients, preferred_element_type=F32)
        kernel_grad = jnp.einsum("ot,co->tc", cot, coefficients, preferred_element_type=F32)
        weighted = kernel_grad * kernel.astype(F32)
        weighted_low = weighted.astype(BF)
        feat_grad_part = -factor * (
            jnp.sum(weighted, axis=1)[:, None] * feat_wide
            - jnp.dot(weighted_low, centers, preferred_element_type=F32)
        )
        center_grad = -factor * (
            jnp.sum(weighted, axis=0)[:, None] * center_wide
            - jnp.einsum("tc,tf->cf", weighted_low, features, preferred_element_type=F32)
        )
        coef_grad = jnp.einsum("tc,ot->co", kernel, cot, preferred_element_type=F32)

        outs = coefficients.shape[1]
        pred_pad = jnp.pad(pred_part, ((0, 0), (0, -outs % 128)))
        carried = jnp.concatenate([feat_grad_part, pred_pad], axis=1)
        for bit in (CORE, X, Y):
            middle = carried.shape[0] // 2
            carried = carried[:middle] + swap(carried[middle:].astype(BF), bit).astype(F32)
        carried = deep_sum(carried)
        feature_grad = carried[:, :feat_width]
        piece = blk // deep
        mine = lax.dynamic_slice_in_dim(carried[:, feat_width:feat_width + outs], depth * piece, piece, 0)
        predictions = lax.ppermute(
            mine.astype(BF), "center", [(i, owner(i)) for i in range(count)]
        ).astype(F32)

        phi_own = (feature_grad * (1.0 - squashed * squashed)).astype(BF)
        phi_grad = ordered(cbit, phi_own, swap(phi_own, CORE), 0)
        second_grad = jnp.dot(hidden, phi_grad, preferred_element_type=F32)
        hidden_grad = jnp.einsum("hf,rf->hr", w_second, phi_grad, preferred_element_type=F32)
        unused, pullback = jax.vjp(jax.nn.gelu, preact)
        preact_grad = pullback(hidden_grad)[0]
        bias_grad = jnp.sum(preact_grad, axis=1, keepdims=True)
        preact_low = preact_grad.astype(BF)
        first_grad = jnp.einsum("hr,dr->hd", preact_low, emb, preferred_element_type=F32)
        grads = jnp.concatenate(
            [first_grad, second_grad, jnp.pad(bias_grad, ((0, 0), (0, 127)))], axis=1
        )
        for bit in (Y, X):
            middle = grads.shape[0] // 2
            grads = grads[:middle] + swap(grads[middle:].astype(BF), bit).astype(F32)
        first_grad = grads[:, :din].T
        second_grad = grads[:, din:din + feat_width]
        bias_grad = grads[:, din + feat_width]
        if groups > 1:
            first_grad, second_grad, center_grad = (
                lax.psum_scatter(first_grad.astype(BF), "dp", scatter_dimension=0, tiled=True).astype(F32),
                lax.psum_scatter(second_grad.astype(BF), "dp", scatter_dimension=1, tiled=True).astype(F32),
                lax.psum_scatter(center_grad.astype(BF), "dp", scatter_dimension=1, tiled=True).astype(F32),
            )
            bias_grad, coef_grad = (
                lax.psum(bias_grad.astype(BF), "dp").astype(F32),
                lax.psum(coef_grad.astype(BF), "dp").astype(F32),
            )
        return (predictions, first_grad, bias_grad, second_grad, center_grad, coef_grad)

    return body


def solution(mesh):
    placed = (
        P("dp", "center"),
        P(None, "center"),
        P("center"),
        P("center", None),
        P("center", None),
        P("center", None),
        P("dp", None),
    )
    return jax.shard_map(
        make_body(mesh.shape["center"], mesh.shape["dp"]),
        mesh=mesh,
        in_specs=placed,
        out_specs=(
            P(("dp", "center"), None),
            P("dp", "center"),
            P("center"),
            P("center", "dp"),
            P("center", "dp"),
            P("center", None),
        ),
        check_vma=False,
    )
```

```python
import jax
import jax.numpy as jnp
from jax import lax
from jax.sharding import PartitionSpec as P

BF = jnp.bfloat16
F32 = jnp.float32
CORE, X, Y, Z = 1, 2, 4, 8


def pick(bit, zero, one):
    return jnp.where(bit == 1, one, zero)


def ordered(bit, own, other, axis):
    return jnp.concatenate([pick(bit, own, other), pick(bit, other, own)], axis=axis)


def arrange(pieces, bits):
    for k, bit in enumerate(bits):
        pieces = [pick(bit, pieces[i], pieces[i ^ (1 << k)]) for i in range(len(pieces))]
    return pieces


def make_body(count, groups):
    deep = count // Z

    def swap(value, bit):
        return lax.ppermute(value, "center", [(i, i ^ bit) for i in range(count)])

    def owner(i):
        block = (i & 1) * 4 + ((i >> 2) & 1) * 2 + ((i >> 1) & 1)
        return deep * block + i // Z

    def body(embeddings, first_weight, first_bias, second_weight, centers, coefficients, cotangent):
        feat_width = centers.shape[1]
        factor = 16.0 / feat_width
        rows = embeddings.shape[0]
        blk = rows // 8
        place = lax.axis_index("center")
        cbit, xbit, ybit, depth = place & 1, (place >> 1) & 1, (place >> 2) & 1, place // Z
        z_bits = [Z << k for k in range(deep.bit_length() - 1)]

        plane = [xbit, ybit]

        cols = embeddings.shape[1]
        local = embeddings.T
        slabs = [
            jnp.concatenate([local[:, (4 * c + p) * blk:][:, :blk] for c in range(2)], axis=1)
            for p in range(4)
        ]
        slabs = arrange(slabs, plane)
        slabs = [slabs[0]] + [swap(slabs[k], k * X) for k in (3, 1, 2)]
        slabs = [slabs[0], slabs[2], slabs[3], slabs[1]]

        hid = first_weight.shape[1]
        high = first_bias.astype(BF)
        low = (first_bias - high.astype(F32)).astype(BF)
        bias_cols = jnp.pad(jnp.stack([high, low], axis=1), ((0, 0), (0, 126)))
        weights = jnp.concatenate([first_weight.T, second_weight, bias_cols], axis=1)
        weights = jnp.concatenate([weights] + [swap(weights, k * X) for k in (1, 2, 3)], axis=0)

        block = jnp.concatenate(arrange(slabs, plane), axis=0)
        layers = [block] + [swap(block, k * Z) for k in range(1, deep)]
        block = jnp.concatenate(arrange(layers, [(depth >> k) & 1 for k in range(len(z_bits))]), axis=0)
        other = swap(block, CORE)
        shape = (4 * deep, 1, cols, 2 * blk)
        emb = ordered(cbit, block.reshape(shape), other.reshape(shape), 1)
        emb = emb.reshape(count * cols, 2 * blk)

        din = first_weight.shape[0]
        w_first = weights[:, :din]
        w_second = weights[:, din:din + feat_width]
        bias = weights[:, din + feat_width:][:, :2].astype(F32).sum(axis=1, keepdims=True)

        preact = jnp.dot(w_first, emb, preferred_element_type=F32) + bias
        hidden = jax.nn.gelu(preact).astype(BF)
        part_sum = jnp.einsum("hr,hf->rf", hidden, w_second, preferred_element_type=F32)
        mine = pick(cbit, part_sum[:blk], part_sum[blk:])
        theirs = pick(cbit, part_sum[blk:], part_sum[:blk])
        total = mine + swap(theirs, CORE)

        def deep_sum(value):
            for bit in z_bits:
                low_value = value.astype(BF)
                value = low_value.astype(F32) + swap(low_value, bit).astype(F32)
            return value

        feature_sum = deep_sum(total)
        squashed = jnp.tanh(feature_sum)
        features = squashed.astype(BF)
        features = jnp.concatenate([features] + [swap(features, k * X) for k in (1, 2, 3)], axis=0)
        features = jnp.concatenate([features, swap(features, CORE)], axis=0)

        cot = cotangent.T
        cot = jnp.concatenate(
            arrange([cot[:, i * blk:][:, :blk] for i in range(8)], [xbit, ybit, cbit]), axis=1
        )

        feat_wide = features.astype(F32)
        center_wide = centers.astype(F32)
        feat_norms = jnp.sum(feat_wide * feat_wide, axis=1)
        center_norms = jnp.sum(center_wide * center_wide, axis=1)
        inner_prods = jnp.einsum("tf,cf->tc", features, centers, preferred_element_type=F32)
        sq_dist = feat_norms[:, None] + center_norms[None, :] - 2.0 * inner_prods
        kernel = jnp.exp(-8.0 * sq_dist / feat_width).astype(BF)
        pred_part = jnp.dot(kernel, coefficients, preferred_element_type=F32)
        kernel_grad = jnp.einsum("ot,co->tc", cot, coefficients, preferred_element_type=F32)
        weighted = kernel_grad * kernel.astype(F32)
        weighted_low = weighted.astype(BF)
        feat_grad_part = -factor * (
            jnp.sum(weighted, axis=1)[:, None] * feat_wide
            - jnp.dot(weighted_low, centers, preferred_element_type=F32)
        )
        center_grad = -factor * (
            jnp.sum(weighted, axis=0)[:, None] * center_wide
            - jnp.einsum("tc,tf->cf", weighted_low, features, preferred_element_type=F32)
        )
        coef_grad = jnp.einsum("tc,ot->co", kernel, cot, preferred_element_type=F32)

        def plane_sum(value):
            middle = value.shape[0] // 2
            value = value[:middle] + swap(value[middle:].astype(BF), CORE).astype(F32)
            low_value = value[blk:].astype(BF)
            parts = [swap(low_value[(k - 1) * blk:][:blk], k * X) for k in (3, 1, 2)]
            return value[:blk] + sum(part.astype(F32) for part in parts)

        feature_grad = deep_sum(plane_sum(feat_grad_part))
        preds = plane_sum(pred_part)
        for k in range(len(z_bits)):
            middle = preds.shape[0] // 2
            bit = (depth >> (len(z_bits) - 1 - k)) & 1
            sent = pick(bit, preds[middle:], preds[:middle]).astype(BF)
            preds = pick(bit, preds[:middle], preds[middle:])
            preds = preds + swap(sent, z_bits[len(z_bits) - 1 - k]).astype(F32)
        predictions = lax.ppermute(
            preds.astype(BF), "center", [(i, owner(i)) for i in range(count)]
        ).astype(F32)

        phi_own = (feature_grad * (1.0 - squashed * squashed)).astype(BF)
        phi_grad = ordered(cbit, phi_own, swap(phi_own, CORE), 0)
        second_grad = jnp.dot(hidden, phi_grad, preferred_element_type=F32)
        hidden_grad = jnp.einsum("hf,rf->hr", w_second, phi_grad, preferred_element_type=F32)
        unused, pullback = jax.vjp(jax.nn.gelu, preact)
        preact_grad = pullback(hidden_grad)[0]
        bias_grad = jnp.sum(preact_grad, axis=1, keepdims=True)
        preact_low = preact_grad.astype(BF)
        hid_blk = first_weight.shape[1]

        def head_grads(k):
            part = slice(k * hid_blk, (k + 1) * hid_blk)
            return jnp.concatenate([
                jnp.einsum("hr,dr->hd", preact_low[part], emb, preferred_element_type=F32),
                second_grad[part],
                jnp.pad(bias_grad[part], ((0, 0), (0, 127))),
            ], axis=1)

        received = [swap(head_grads(k).astype(BF), k * X) for k in (3, 1, 2)]
        grads = head_grads(0) + sum(part.astype(F32) for part in received)
        first_grad = grads[:, :din].T
        second_grad = grads[:, din:din + feat_width]
        bias_grad = grads[:, din + feat_width]
        if groups > 1:
            first_grad, second_grad, center_grad = (
                lax.psum_scatter(first_grad.astype(BF), "dp", scatter_dimension=0, tiled=True).astype(F32),
                lax.psum_scatter(second_grad.astype(BF), "dp", scatter_dimension=1, tiled=True).astype(F32),
                lax.psum_scatter(center_grad.astype(BF), "dp", scatter_dimension=1, tiled=True).astype(F32),
            )
            bias_grad, coef_grad = (
                lax.psum(bias_grad.astype(BF), "dp").astype(F32),
                lax.psum(coef_grad.astype(BF), "dp").astype(F32),
            )
        return (predictions, first_grad, bias_grad, second_grad, center_grad, coef_grad)

    return body


def solution(mesh):
    placed = (
        P("dp", "center"),
        P(None, "center"),
        P("center"),
        P("center", None),
        P("center", None),
        P("center", None),
        P("dp", None),
    )
    return jax.shard_map(
        make_body(mesh.shape["center"], mesh.shape["dp"]),
        mesh=mesh,
        in_specs=placed,
        out_specs=(
            P(("dp", "center"), None),
            P("dp", "center"),
            P("center"),
            P("center", "dp"),
            P("center", "dp"),
            P("center", None),
        ),
        check_vma=False,
    )
```

```python
import jax
import jax.numpy as jnp
from jax import lax
from jax.experimental import pallas as pl
from jax.experimental.pallas import tpu as pltpu
from jax.sharding import PartitionSpec as P


BF = jnp.bfloat16
F32 = jnp.float32
CORE, X, Y, Z = 1, 2, 4, 8
ROOM = {"head": 8, "main": 16, "far": 12, "near": 12, "bwd": 8, "join": 4, "again": 8}


def pick(bit, zero, one):
    return jnp.where(bit == 1, one, zero)


def arrange(pieces, bits):
    for k, bit in enumerate(bits):
        pieces = [pick(bit, pieces[i], pieces[i ^ (1 << k)]) for i in range(len(pieces))]
    return pieces


def nt_dot(a, b):
    return lax.dot_general(a, b, (((1,), (1,)), ((), ())), preferred_element_type=F32)


def tn_dot(a, b):
    return lax.dot_general(a, b, (((0,), (0,)), ((), ())), preferred_element_type=F32)


VM = pl.BlockSpec(memory_space=pltpu.VMEM)
SM = pl.BlockSpec(memory_space=pltpu.SMEM)


def local_call(kernel, shapes, scratch=(), flops=0, moved=0, smem=0, operands=(), room=16, keep=True):
    return pl.pallas_call(
        kernel,
        in_specs=[SM] * smem + [VM] * (len(operands) - smem),
        out_specs=[VM] * len(shapes),
        out_shape=[(pltpu.VMEM if keep else jax.ShapeDtypeStruct)(shape, dtype) for shape, dtype in shapes],
        scratch_shapes=list(scratch),
        cost_estimate=pl.CostEstimate(flops=flops, bytes_accessed=moved, transcendentals=0),
        compiler_params=pltpu.CompilerParams(vmem_limit_bytes=room << 20),
    )(*operands)


def join(parts, target):
    step = parts[0].shape[0]
    for i, part in enumerate(parts):
        target[i * step:(i + 1) * step, :] = part[...]


def cot_pass(place, cot):
    outs, rows = cot.shape
    blk = rows // 8

    def kernel(place_ref, cot_ref, cols_out, rows_out):
        here = place_ref[0]
        core, plane = here % 2, (here // 2) % 4
        for k in range(4):
            at = pl.multiple_of((4 * core + (plane ^ k)) * blk, blk)
            cols_out[:, k * blk:(k + 1) * blk] = cot_ref[:, pl.ds(at, blk)]
        shape = (outs, outs)
        same = lax.broadcasted_iota(jnp.int32, shape, 0) == lax.broadcasted_iota(jnp.int32, shape, 1)
        rows_out[...] = tn_dot(cols_out[...], jnp.where(same, 1.0, 0.0).astype(BF)).astype(BF)

    return local_call(
        kernel, [((outs, 4 * blk), BF), ((4 * blk, outs), BF)], smem=1, moved=4 * outs * rows,
        operands=(place, cot), room=4,
    )


def pred_step(place, parts, level):
    rows, outs = parts[0].shape
    half = rows // 2

    def kernel(place_ref, *refs):
        *ins, keep, sent, total = refs
        value = ins[0][...]
        for ref in ins[1:]:
            value = value + ref[...].astype(F32)
        total[...] = value
        bit = (place_ref[0] // (Z << level)) % 2
        keep[...] = total[pl.ds(pl.multiple_of(bit * half, half), half), :]
        sent[...] = total[pl.ds(pl.multiple_of((1 - bit) * half, half), half), :].astype(BF)

    return local_call(
        kernel, [((half, outs), F32), ((half, outs), BF)], [pltpu.VMEM((rows, outs), F32)],
        smem=1, moved=8 * rows * outs, operands=(place, *parts), room=2,
    )


def head_pass(place, weights, own, other, width, count):
    hid = weights[0].shape[0]
    pieces, rows = own.shape
    din, half, cols = 2 * pieces, rows // 2, 2 * pieces // count

    def kernel(place_ref, w0, w1, w2, w3, own_ref, other_ref, mine, theirs, emb_out, emb, first, second):
        here = place_ref[0]
        core, plane, depth = here % 2, (here // 2) % 4, here // Z
        for k in range(pieces // cols):
            source = (depth ^ (k // 4)) * Z + (plane ^ (k % 4)) * 2
            part = slice(k * cols, (k + 1) * cols)
            for ref, which in ((own_ref, core), (other_ref, 1 - core)):
                at = pl.multiple_of((source + which) * cols, cols)
                emb[pl.ds(at, cols), :] = ref[part, :]
        parts = (w0, w1, w2, w3)
        for i, part in enumerate(parts):
            first[i * hid:(i + 1) * hid, :] = part[:, :din]
            second[i * hid:(i + 1) * hid, :] = part[:, din:din + width]
        bias = jnp.concatenate(
            [jnp.sum(part[:, din + width:].astype(F32), axis=1, keepdims=True) for part in parts], axis=0
        )
        preact = jnp.dot(first[...], emb[...], preferred_element_type=F32) + bias
        hidden = jax.nn.gelu(preact).astype(BF)
        sums = tn_dot(hidden, second[...])

        @pl.when(core == 0)
        def _():
            mine[...] = sums[:half]
            theirs[...] = sums[half:]
            emb_out[...] = emb[:, :half]

        @pl.when(core == 1)
        def _():
            mine[...] = sums[half:]
            theirs[...] = sums[:half]
            emb_out[...] = emb[:, half:]

    return local_call(
        kernel, [((half, width), F32)] * 2 + [((din, half), BF)],
        [pltpu.VMEM((din, rows), BF), pltpu.VMEM((4 * hid, din), BF), pltpu.VMEM((4 * hid, width), BF)],
        flops=8 * hid * rows * (din + width), moved=8 * hid * din, smem=1,
        operands=(place, *weights, own, other), room=ROOM["head"],
    )


def point_pass(feats, cot, sets, norms, factor, tile=512):
    blk, width = feats[0].shape
    rows, points, outs = 4 * blk, sets[0][0].shape[0], cot.shape[1]
    tile = min(tile, points)
    scale = -8.0 / width

    def kernel(f0, f1, f2, f3, cot_ref, cen0, cen1, coef0, coef1, norm0, norm1,
               kern0, kern1, low0, low1, col0, col1, grad0, grad1, grad2, grad3, fs, acc):
        join((f0, f1, f2, f3), fs)
        wide = fs[...].astype(F32)
        feat_norm = scale * jnp.sum(wide * wide, axis=1, keepdims=True)
        acc[...] = jnp.zeros_like(acc)
        lanes = acc.shape[1]
        for cen, coef, norm, kern_out, low_out, col_out in (
            (cen0, coef0, norm0, kern0, low0, col0), (cen1, coef1, norm1, kern1, low1, col1)
        ):
            @pl.loop(0, points // tile)
            def _(i):
                at = pl.ds(pl.multiple_of(i * tile, tile), tile)
                inner = nt_dot(fs[...], cen[at, :])
                grad = jnp.dot(cot_ref[...], coef[:, at], preferred_element_type=F32)
                shift = feat_norm + scale * norm[:, at]
                kern = jnp.exp((-2.0 * scale) * inner + shift).astype(BF)
                weighted = grad * kern.astype(F32)
                kern_out[:, at] = kern
                low_out[:, at] = weighted.astype(BF)
                col_out[:, at] = jnp.sum(weighted, axis=0, keepdims=True)
                acc[...] += sum(weighted[:, k * lanes:(k + 1) * lanes] for k in range(tile // lanes))

        sums = jnp.sum(acc[...], axis=1, keepdims=True)
        grad = jnp.dot(low0[...], cen0[...], preferred_element_type=F32)
        grad = grad + jnp.dot(low1[...], cen1[...], preferred_element_type=F32)
        grad = -factor * (sums * fs[...].astype(F32) - grad)
        for k, out in enumerate((grad0, grad1, grad2, grad3)):
            out[...] = grad[k * blk:(k + 1) * blk].astype(out.dtype)

    return local_call(
        kernel,
        [((rows, points), BF)] * 4 + [((1, points), F32)] * 2 + [((blk, width), F32)] + [((blk, width), BF)] * 3,
        [pltpu.VMEM((rows, width), BF), pltpu.VMEM((rows, 128), F32)],
        flops=8 * rows * points * (width + outs), moved=16 * rows * points,
        operands=(*feats, cot, sets[0][0], sets[1][0], sets[0][1], sets[1][1], *norms), room=ROOM["main"],
    )


def far_points(feats, cot, kerns, lows, col, points_ref, coefs, factor, tile=512):
    blk, width = feats[0].shape
    rows, points, outs = 4 * blk, kerns[0].shape[1], cot.shape[0]
    tile = min(tile, points)

    def kernel(f0, f1, f2, f3, cot_ref, kern0, kern1, low, col_ref, cen, coef0, coef1, cen_out, coef_out, pred0, pred1, pred2, pred3, fs):
        join((f0, f1, f2, f3), fs)
        total = nt_dot(kern0[...], coef0[...]) + nt_dot(kern1[...], coef1[...])
        for k, out in enumerate((pred0, pred1, pred2, pred3)):
            out[...] = total[k * blk:(k + 1) * blk].astype(out.dtype)

        @pl.loop(0, points // tile)
        def _(i):
            at = pl.ds(pl.multiple_of(i * tile, tile), tile)
            sums = jnp.broadcast_to(col_ref[:, at], (128, tile)).T[:, :1]
            part = tn_dot(low[:, at], fs[...])
            cen_out[at, :] = (-factor * (sums * cen[at, :].astype(F32) - part)).astype(BF)
            coef_out[:, at] = jnp.dot(cot_ref[...], kern1[:, at], preferred_element_type=F32).astype(BF)

    return local_call(
        kernel, [((points, width), BF), ((outs, points), BF), ((blk, outs), F32)] + [((blk, outs), BF)] * 3,
        [pltpu.VMEM((rows, width), BF)],
        flops=2 * rows * points * (width + 3 * outs), moved=4 * rows * points,
        operands=(*feats, cot, *kerns, lows, col, points_ref, *coefs), room=ROOM["far"],
    )


def near_points(feats, cot, kern, low, col, points_ref, got_cen, got_coef, factor, tile=512):
    blk, width = feats[0].shape
    rows, points, outs = 4 * blk, kern.shape[1], cot.shape[0]
    tile = min(tile, points)

    def kernel(f0, f1, f2, f3, cot_ref, kern_ref, low_ref, col_ref, cen, got_c, got_k, cen_out, coef_out, fs):
        @pl.when(pl.program_id(0) == 0)
        def _():
            join((f0, f1, f2, f3), fs)

        at = pl.ds(pl.multiple_of(pl.program_id(0) * tile, tile), tile)
        sums = jnp.broadcast_to(col_ref[:, at], (128, tile)).T[:, :1]
        part = tn_dot(low_ref[:, at], fs[...])
        cen_out[...] = -factor * (sums * cen[at, :].astype(F32) - part) + got_c[at, :].astype(F32)
        coef_out[...] = (
            jnp.dot(cot_ref[...], kern_ref[:, at], preferred_element_type=F32) + got_k[:, at].astype(F32)
        )

    by_row = lambda n: pl.BlockSpec((tile, n), lambda i: (i, 0))
    by_col = lambda n: pl.BlockSpec((n, tile), lambda i: (0, i))
    return pl.pallas_call(
        kernel,
        grid=(points // tile,),
        in_specs=[VM] * 11,
        out_specs=[by_row(width), by_col(outs)],
        out_shape=[jax.ShapeDtypeStruct((points, width), F32), jax.ShapeDtypeStruct((outs, points), F32)],
        scratch_shapes=[pltpu.VMEM((rows, width), BF)],
        cost_estimate=pl.CostEstimate(
            flops=2 * rows * points * (width + outs), bytes_accessed=4 * rows * points, transcendentals=0
        ),
        compiler_params=pltpu.CompilerParams(vmem_limit_bytes=ROOM["near"] << 20),
    )(*feats, cot, kern, low, col, points_ref, got_cen, got_coef)


def head_again(own, other, embs, width):
    hid = own.shape[0]
    din, blk = embs[0].shape
    rows = 4 * blk

    def kernel(own_ref, other_ref, e0, e1, e2, e3, hidden_out, slope_out, second_out, emb_out, first):
        for k, ref in enumerate((e0, e1, e2, e3)):
            emb_out[:, k * blk:(k + 1) * blk] = ref[...]
        for k, ref in enumerate((own_ref, other_ref)):
            first[k * hid:(k + 1) * hid, :] = ref[:, :din]
            second_out[k * hid:(k + 1) * hid, :] = ref[:, din:din + width]
        bias = jnp.concatenate([
            jnp.sum(ref[:, din + width:].astype(F32), axis=1, keepdims=True) for ref in (own_ref, other_ref)
        ], axis=0)
        preact = jnp.dot(first[...], emb_out[...], preferred_element_type=F32) + bias
        hidden, pullback = jax.vjp(jax.nn.gelu, preact)
        hidden_out[...] = hidden.astype(BF)
        slope_out[...] = pullback(jnp.ones_like(preact))[0]

    return local_call(
        kernel,
        [((2 * hid, rows), BF), ((2 * hid, rows), F32), ((2 * hid, width), BF), ((din, rows), BF)],
        [pltpu.VMEM((2 * hid, din), BF)],
        flops=4 * hid * rows * din, moved=4 * rows * din,
        operands=(own, other, *embs), room=ROOM["again"],
    )


def head_grads(phis, hidden, slope, second, emb):
    _, width = phis[0].shape
    din, rows = emb.shape
    hid = hidden.shape[0] // 2

    def kernel(p0, p1, p2, p3, hid_ref, slope_ref, w_ref, emb_ref, first_out, second_out, bias_out, sent, phi):
        join((p0, p1, p2, p3), phi)
        grad = nt_dot(w_ref[...], phi[...]) * slope_ref[...]
        low = grad.astype(BF)
        rest = (grad - low.astype(F32)).astype(BF)
        ones = jnp.ones((16, rows), BF)
        firsts = nt_dot(low, emb_ref[...])
        seconds = jnp.dot(hid_ref[...], phi[...], preferred_element_type=F32)
        first_out[...] = firsts[:hid]
        second_out[...] = seconds[:hid]
        bias_out[...] = nt_dot(ones, low[:hid]) + nt_dot(ones, rest[:hid])
        sent[:hid, :din] = firsts[hid:].astype(BF)
        sent[:hid, din:] = seconds[hid:].astype(BF)
        sent[hid:, :] = jnp.zeros((16, din + width), BF)
        sent[hid:, :hid] = (nt_dot(ones, low[hid:]) + nt_dot(ones, rest[hid:])).astype(BF)

    return local_call(
        kernel,
        [((hid, din), F32), ((hid, width), F32), ((16, hid), F32), ((hid + 16, din + width), BF)],
        [pltpu.VMEM((rows, width), BF)],
        flops=4 * hid * rows * (din + 2 * width), moved=4 * rows * din,
        operands=(*phis, hidden, slope, second, emb), room=ROOM["bwd"],
    )


def head_join(first, second, bias, got):
    hid, din = first.shape

    def kernel(first_ref, second_ref, bias_ref, got_ref, first_out, second_out, bias_out):
        first_out[...] = first_ref[...] + got_ref[:hid, :din].astype(F32)
        second_out[...] = second_ref[...] + got_ref[:hid, din:].astype(F32)
        bias_out[...] = bias_ref[:1, :] + got_ref[hid:, :hid][:1, :].astype(F32)

    return local_call(
        kernel, [(first.shape, F32), (second.shape, F32), ((1, hid), F32)],
        moved=12 * hid * din, operands=(first, second, bias, got), room=ROOM["join"], keep=False,
    )


def make_body(count, groups):
    deep = count // Z
    levels = deep.bit_length() - 1

    def send(value, pairs):
        return lax.ppermute(value, "center", pairs)

    def swap(value, bit):
        return send(value, [(i, i ^ bit) for i in range(count)])

    def owner(i):
        block = (i & 1) * 4 + ((i >> 1) & 3)
        return deep * block + i // Z

    def inner_body(embeddings, first_weight, first_bias, second_weight, centers, coefficients, cotangent):
        feat_width = centers.shape[1]
        factor = 16.0 / feat_width
        rows = embeddings.shape[0]
        blk = rows // 8
        _, hid = first_weight.shape
        place = lax.axis_index("center")
        xbit, ybit = (place >> 1) & 1, (place >> 2) & 1
        plane = [xbit, ybit]

        local = embeddings.T
        slabs = [
            jnp.concatenate([local[:, (4 * c + p) * blk:][:, :blk] for c in range(2)], axis=1)
            for p in range(4)
        ]
        slabs = arrange(slabs, plane)
        got = {k: swap(slabs[k], k * X) for k in (3, 1, 2)}
        block = jnp.concatenate([slabs[0], got[1], got[2], got[3]], axis=0)

        high = first_bias.astype(BF)
        low = (first_bias - high.astype(F32)).astype(BF)
        spread = jnp.concatenate([high, low])
        hids = lax.broadcasted_iota(jnp.int32, (hid, 2 * hid), 0)
        slots = lax.broadcasted_iota(jnp.int32, (hid, 2 * hid), 1) % hid
        bias_cols = jnp.where(hids == slots, spread[None, :], jnp.zeros((), BF))
        bias_cols = jnp.pad(bias_cols, ((0, 0), (0, -2 * hid % 128)))
        own_weights = jnp.concatenate([first_weight.T, second_weight, bias_cols], axis=1)
        got = {k: swap(own_weights, k * X) for k in (3, 1, 2)}
        weights = [own_weights, got[1], got[2], got[3]]
        core_weights = swap(own_weights, CORE)

        block = jnp.concatenate([block] + [swap(block, k * Z) for k in range(1, deep)], axis=0)
        other = swap(block, CORE)
        mine, theirs, emb_own = head_pass(place[None], weights, block, other, feat_width, count)
        total = mine + swap(theirs, CORE)

        def deep_sum(value):
            for k in range(levels):
                low_value = value.astype(BF)
                value = low_value.astype(F32) + swap(low_value, Z << k).astype(F32)
            return value

        feature_sum = deep_sum(total)
        squashed = jnp.tanh(feature_sum)
        own_feats = squashed.astype(BF)
        got = {k: swap(own_feats, k * X) for k in (3, 1, 2)}

        cot, cot_rows = cot_pass(place[None], cotangent.T)

        emb_x, emb_y = swap(emb_own, X), swap(emb_own, Y)
        emb_xy = swap(emb_y, X)

        coef_own = coefficients.T
        sets = [
            (centers, coef_own),
            (swap(centers, CORE), swap(coef_own, CORE)),
        ]
        norms = []
        for points, coef in sets:
            wide = points.astype(F32)
            norms.append(jnp.sum(wide * wide, axis=1)[None, :])
        feats = [own_feats, got[1], got[2], got[3]]
        kern0, kern1, low0, low1, col0, col1, *grads = point_pass(feats, cot_rows, sets, norms, factor)

        def plane_sum(parts):
            got = [swap(parts[k], k * X) for k in (3, 1, 2)]
            return parts[0].astype(F32) + sum(part.astype(F32) for part in got)

        feature_grad = deep_sum(plane_sum(grads))
        phi_own = (feature_grad * (1.0 - squashed * squashed)).astype(BF)
        got = {k: swap(phi_own, k * X) for k in (3, 1, 2)}
        phis = [phi_own, got[1], got[2], got[3]]

        far_cen, far_coef, *preds = far_points(
            feats, cot, (kern0, kern1), low1, col1, sets[1][0], (sets[0][1], sets[1][1]), factor
        )
        got = {k: swap(preds[k], k * X) for k in (3, 1, 2)}
        parts = [preds[0], got[1], got[2], got[3]]
        for k in reversed(range(levels)):
            keep, sent = pred_step(place[None], parts, k)
            parts = [keep, swap(sent, Z << k)]
        preds = sum(part.astype(F32) for part in parts)
        predictions = send(preds.astype(BF), [(i, owner(i)) for i in range(count)]).astype(F32)

        got_cen, got_coef = swap(far_cen, CORE), swap(far_coef, CORE)
        center_grad, coef_grad = near_points(
            feats, cot, kern0, low0, col0, centers, got_cen, got_coef, factor
        )
        coef_grad = coef_grad.T

        hidden, slope, second, emb_rows = head_again(
            own_weights, core_weights, [emb_own, emb_x, emb_y, emb_xy], feat_width
        )
        first_grad, second_grad, bias_grad, sent = head_grads(phis, hidden, slope, second, emb_rows)
        got = swap(sent, CORE)
        first_grad, second_grad, bias_grad = head_join(first_grad, second_grad, bias_grad, got)
        first_grad = first_grad.T
        bias_grad = bias_grad[0]
        if groups > 1:
            first_grad, second_grad, center_grad = (
                lax.psum_scatter(first_grad.astype(BF), "dp", scatter_dimension=0, tiled=True).astype(F32),
                lax.psum_scatter(second_grad.astype(BF), "dp", scatter_dimension=1, tiled=True).astype(F32),
                lax.psum_scatter(center_grad.astype(BF), "dp", scatter_dimension=1, tiled=True).astype(F32),
            )
            bias_grad, coef_grad = (
                lax.psum(bias_grad.astype(BF), "dp").astype(F32),
                lax.psum(coef_grad.astype(BF), "dp").astype(F32),
            )
        return (predictions, first_grad, bias_grad, second_grad, center_grad, coef_grad)

    return inner_body


def solution(mesh):
    placed = (
        P("dp", "center"),
        P(None, "center"),
        P("center"),
        P("center", None),
        P("center", None),
        P("center", None),
        P("dp", None),
    )
    count, groups = mesh.shape["center"], mesh.shape["dp"]
    return jax.shard_map(
        make_body(count, groups),
        mesh=mesh,
        in_specs=placed,
        out_specs=(
            P(("dp", "center"), None),
            P("dp", "center"),
            P("center"),
            P("center", "dp"),
            P("center", "dp"),
            P("center", None),
        ),
        check_vma=False,
    )
```

```python
import math

import jax
import jax.numpy as jnp
from jax import lax
from jax.experimental import pallas as pl
from jax.experimental.pallas import tpu as pltpu
from jax.sharding import PartitionSpec as P


BF = jnp.bfloat16
F32 = jnp.float32
CORE, X, Y, Z = 1, 2, 4, 8
ROOM = {"head": 8, "main": 16, "far": 12, "near": 12, "bwd": 8, "join": 4, "again": 8}


def pick(bit, zero, one):
    return jnp.where(bit == 1, one, zero)


def arrange(pieces, bits):
    for k, bit in enumerate(bits):
        pieces = [pick(bit, pieces[i], pieces[i ^ (1 << k)]) for i in range(len(pieces))]
    return pieces


def nt_dot(a, b):
    return lax.dot_general(a, b, (((1,), (1,)), ((), ())), preferred_element_type=F32)


def tn_dot(a, b):
    return lax.dot_general(a, b, (((0,), (0,)), ((), ())), preferred_element_type=F32)


VM = pl.BlockSpec(memory_space=pltpu.VMEM)
SM = pl.BlockSpec(memory_space=pltpu.SMEM)


def local_call(kernel, shapes, scratch=(), flops=0, moved=0, smem=0, operands=(), room=16, keep=True):
    return pl.pallas_call(
        kernel,
        in_specs=[SM] * smem + [VM] * (len(operands) - smem),
        out_specs=[VM] * len(shapes),
        out_shape=[(pltpu.VMEM if keep else jax.ShapeDtypeStruct)(shape, dtype) for shape, dtype in shapes],
        scratch_shapes=list(scratch),
        cost_estimate=pl.CostEstimate(flops=flops, bytes_accessed=moved, transcendentals=0),
        compiler_params=pltpu.CompilerParams(vmem_limit_bytes=room << 20),
    )(*operands)


def join(parts, target):
    step = parts[0].shape[0]
    for i, part in enumerate(parts):
        target[i * step:(i + 1) * step, :] = part[...]


def cot_pass(place, cot):
    outs, rows = cot.shape
    blk = rows // 8

    def kernel(place_ref, cot_ref, cols_out, rows_out):
        here = place_ref[0]
        core, plane = here % 2, (here // 2) % 4
        for k in range(4):
            at = pl.multiple_of((4 * core + (plane ^ k)) * blk, blk)
            cols_out[:, k * blk:(k + 1) * blk] = cot_ref[:, pl.ds(at, blk)]
        shape = (outs, outs)
        same = lax.broadcasted_iota(jnp.int32, shape, 0) == lax.broadcasted_iota(jnp.int32, shape, 1)
        rows_out[...] = tn_dot(cols_out[...], jnp.where(same, 1.0, 0.0).astype(BF)).astype(BF)

    return local_call(
        kernel, [((outs, 4 * blk), BF), ((4 * blk, outs), BF)], smem=1, moved=4 * outs * rows,
        operands=(place, cot), room=4,
    )


def pred_step(place, parts, level):
    rows, outs = parts[0].shape
    half = rows // 2

    def kernel(place_ref, *refs):
        *ins, keep, sent, total = refs
        value = ins[0][...]
        for ref in ins[1:]:
            value = value + ref[...].astype(F32)
        total[...] = value
        bit = (place_ref[0] // (Z << level)) % 2
        keep[...] = total[pl.ds(pl.multiple_of(bit * half, half), half), :]
        sent[...] = total[pl.ds(pl.multiple_of((1 - bit) * half, half), half), :].astype(BF)

    return local_call(
        kernel, [((half, outs), F32), ((half, outs), BF)], [pltpu.VMEM((rows, outs), F32)],
        smem=1, moved=8 * rows * outs, operands=(place, *parts), room=2,
    )


def head_pass(place, weights, own, other, order, width, count):
    hid = weights[0].shape[0]
    share, rows = own[0].shape
    deep, size = len(own), len(other)
    din, half = 2 * share * deep, rows // 2
    cols = din // count

    def kernel(place_ref, w0, w1, w2, w3, *refs):
        own_refs, other_refs = refs[:deep], refs[deep:deep + size]
        mine, theirs, emb_out, emb, first, second = refs[deep + size:]
        here = place_ref[0]
        core, plane, depth = here % 2, (here // 2) % 4, here // Z
        pieces = [(level, ref, 0, core) for level, ref in enumerate(own_refs)]
        for ref, levels in zip(other_refs, order):
            pieces += [(level, ref, i * share, 1 - core) for i, level in enumerate(levels)]
        for level, ref, base, which in pieces:
            for k in range(4):
                source = (depth ^ level) * Z + (plane ^ k) * 2 + which
                at = pl.ds(pl.multiple_of(source * cols, cols), cols)
                emb[at, :] = ref[base + k * cols:base + (k + 1) * cols, :]
        parts = (w0, w1, w2, w3)
        for i, part in enumerate(parts):
            first[i * hid:(i + 1) * hid, :] = part[:, :din]
            second[i * hid:(i + 1) * hid, :] = part[:, din:din + width]
        bias = jnp.concatenate(
            [jnp.sum(part[:, din + width:].astype(F32), axis=1, keepdims=True) for part in parts], axis=0
        )
        preact = jnp.dot(first[...], emb[...], preferred_element_type=F32) + bias
        hidden = jax.nn.gelu(preact).astype(BF)
        sums = tn_dot(hidden, second[...])

        @pl.when(core == 0)
        def _():
            mine[...] = sums[:half]
            theirs[...] = sums[half:]
            emb_out[...] = emb[:, :half]

        @pl.when(core == 1)
        def _():
            mine[...] = sums[half:]
            theirs[...] = sums[:half]
            emb_out[...] = emb[:, half:]

    return local_call(
        kernel, [((half, width), F32)] * 2 + [((din, half), BF)],
        [pltpu.VMEM((din, rows), BF), pltpu.VMEM((4 * hid, din), BF), pltpu.VMEM((4 * hid, width), BF)],
        flops=8 * hid * rows * (din + width), moved=8 * hid * din, smem=1,
        operands=(place, *weights, *own, *other), room=ROOM["head"],
    )


def slope_pass(cot, coefs, tile=512):
    rows, outs = cot.shape
    points = coefs[0].shape[1]
    tile = min(tile, points)

    half = rows // 2

    def kernel(cot_ref, coef0, coef1, out0, out1, out2, out3):
        for coef, near, far in ((coef0, out0, out2), (coef1, out1, out3)):
            @pl.loop(0, points // tile)
            def _(i):
                at = pl.ds(pl.multiple_of(i * tile, tile), tile)
                value = jnp.dot(cot_ref[...], coef[:, at], preferred_element_type=F32)
                near[:, at] = value[:half]
                far[:, at] = value[half:]

    return local_call(
        kernel, [((half, points), F32)] * 4, flops=4 * rows * points * outs, moved=8 * rows * points,
        operands=(cot, *coefs), room=4,
    )


def point_pass(feats, slopes, sets, norms, factor, kinds, tile=512):
    blk, width = feats[0].shape
    count, points = len(feats), sets[0][0].shape[0]
    rows = count * blk
    tile = min(tile, points)
    scale = -8.0 / width * math.log2(math.e)

    def kernel(*refs):
        cen0, cen1, slope0, slope1, norm0, norm1, kern0, kern1, low0, low1, col0, col1 = refs[count:count + 12]
        outs, (fs, acc) = refs[count + 12:-2], refs[-2:]
        join(refs[:count], fs)
        wide = fs[...].astype(F32)
        feat_norm = scale * jnp.sum(wide * wide, axis=1, keepdims=True)
        acc[...] = jnp.zeros_like(acc)
        lanes = acc.shape[1]
        for cen, slope, norm, kern_out, low_out, col_out in (
            (cen0, slope0, norm0, kern0, low0, col0), (cen1, slope1, norm1, kern1, low1, col1)
        ):
            @pl.loop(0, points // tile, unroll=True)
            def _(i):
                at = pl.ds(pl.multiple_of(i * tile, tile), tile)
                inner = nt_dot(fs[...], cen[at, :])
                shift = feat_norm + scale * norm[:, at]
                kern = jnp.exp2((-2.0 * scale) * inner + shift).astype(BF)
                weighted = slope[:, at] * kern.astype(F32)
                kern_out[:, at] = kern
                low_out[:, at] = weighted.astype(BF)
                col_out[:, at] = jnp.sum(weighted, axis=0, keepdims=True)
                acc[...] += sum(weighted[:, k * lanes:(k + 1) * lanes] for k in range(tile // lanes))

        sums = jnp.sum(acc[...], axis=1, keepdims=True)
        grad = jnp.dot(low0[...], cen0[...], preferred_element_type=F32)
        grad = grad + jnp.dot(low1[...], cen1[...], preferred_element_type=F32)
        grad = -factor * (sums * fs[...].astype(F32) - grad)
        for k, out in enumerate(outs):
            out[...] = grad[k * blk:(k + 1) * blk].astype(out.dtype)

    return local_call(
        kernel,
        [((rows, points), BF)] * 4 + [((1, points), F32)] * 2 + [((blk, width), dtype) for dtype in kinds],
        [pltpu.VMEM((rows, width), BF), pltpu.VMEM((rows, 128), F32)],
        flops=8 * rows * points * width, moved=16 * rows * points,
        operands=(*feats, sets[0][0], sets[1][0], *slopes, *norms), room=ROOM["main"],
    )


def far_points(feats, cot, kerns, lows, col, points_ref, coefs, factor, tile=512):
    blk, width = feats[0].shape
    rows, points, outs = 4 * blk, kerns[0][0].shape[1], cot.shape[0]
    half = rows // 2
    tile = min(tile, points)

    def kernel(f0, f1, f2, f3, cot_ref, kern0a, kern0b, kern1a, kern1b, lowa, lowb, cola, colb, cen, coef0, coef1,
               cen_out, coef_out, pred0, pred1, pred2, pred3, fs):
        join((f0, f1, f2, f3), fs)
        for first, second, out0, out1 in ((kern0a, kern1a, pred0, pred1), (kern0b, kern1b, pred2, pred3)):
            total = nt_dot(first[...], coef0[...]) + nt_dot(second[...], coef1[...])
            out0[...] = total[:blk].astype(out0.dtype)
            out1[...] = total[blk:].astype(out1.dtype)

        @pl.loop(0, points // tile)
        def _(i):
            at = pl.ds(pl.multiple_of(i * tile, tile), tile)
            sums = jnp.broadcast_to(cola[:, at] + colb[:, at], (128, tile)).T[:, :1]
            part = tn_dot(lowa[:, at], fs[:half, :]) + tn_dot(lowb[:, at], fs[half:, :])
            cen_out[at, :] = (-factor * (sums * cen[at, :].astype(F32) - part)).astype(BF)
            coef_out[:, at] = (
                jnp.dot(cot_ref[:, :half], kern1a[:, at], preferred_element_type=F32)
                + jnp.dot(cot_ref[:, half:], kern1b[:, at], preferred_element_type=F32)
            ).astype(BF)

    return local_call(
        kernel, [((points, width), BF), ((outs, points), BF), ((blk, outs), F32)] + [((blk, outs), BF)] * 3,
        [pltpu.VMEM((rows, width), BF)],
        flops=2 * rows * points * (width + 3 * outs), moved=4 * rows * points,
        operands=(*feats, cot, *kerns[0], *kerns[1], *lows, *col, points_ref, *coefs), room=ROOM["far"],
    )


def near_points(feats, cot, kern, low, col, points_ref, got_cen, got_coef, factor, tile=512):
    blk, width = feats[0].shape
    rows, points, outs = 4 * blk, kern[0].shape[1], cot.shape[0]
    half = rows // 2
    tile = min(tile, points)

    def kernel(f0, f1, f2, f3, cot_ref, kerna, kernb, lowa, lowb, cola, colb, cen, got_c, got_k, cen_out, coef_out, fs):
        @pl.when(pl.program_id(0) == 0)
        def _():
            join((f0, f1, f2, f3), fs)

        at = pl.ds(pl.multiple_of(pl.program_id(0) * tile, tile), tile)
        sums = jnp.broadcast_to(cola[:, at] + colb[:, at], (128, tile)).T[:, :1]
        part = tn_dot(lowa[:, at], fs[:half, :]) + tn_dot(lowb[:, at], fs[half:, :])
        cen_out[...] = -factor * (sums * cen[at, :].astype(F32) - part) + got_c[at, :].astype(F32)
        coef_out[...] = (
            jnp.dot(cot_ref[:, :half], kerna[:, at], preferred_element_type=F32)
            + jnp.dot(cot_ref[:, half:], kernb[:, at], preferred_element_type=F32)
            + got_k[:, at].astype(F32)
        )

    by_row = lambda n: pl.BlockSpec((tile, n), lambda i: (i, 0))
    by_col = lambda n: pl.BlockSpec((n, tile), lambda i: (0, i))
    return pl.pallas_call(
        kernel,
        grid=(points // tile,),
        in_specs=[VM] * 14,
        out_specs=[by_row(width), by_col(outs)],
        out_shape=[jax.ShapeDtypeStruct((points, width), F32), jax.ShapeDtypeStruct((outs, points), F32)],
        scratch_shapes=[pltpu.VMEM((rows, width), BF)],
        cost_estimate=pl.CostEstimate(
            flops=2 * rows * points * (width + outs), bytes_accessed=4 * rows * points, transcendentals=0
        ),
        compiler_params=pltpu.CompilerParams(vmem_limit_bytes=ROOM["near"] << 20),
    )(*feats, cot, *kern, *low, *col, points_ref, got_cen, got_coef)


def head_again(own, other, embs, width):
    hid = own.shape[0]
    din, blk = embs[0].shape
    rows = 4 * blk

    def kernel(own_ref, other_ref, e0, e1, e2, e3, hidden_out, slope_out, second_out, emb_out, first):
        for k, ref in enumerate((e0, e1, e2, e3)):
            emb_out[:, k * blk:(k + 1) * blk] = ref[...]
        for k, ref in enumerate((own_ref, other_ref)):
            first[k * hid:(k + 1) * hid, :] = ref[:, :din]
            second_out[k * hid:(k + 1) * hid, :] = ref[:, din:din + width]
        bias = jnp.concatenate([
            jnp.sum(ref[:, din + width:].astype(F32), axis=1, keepdims=True) for ref in (own_ref, other_ref)
        ], axis=0)
        preact = jnp.dot(first[...], emb_out[...], preferred_element_type=F32) + bias
        hidden, pullback = jax.vjp(jax.nn.gelu, preact)
        hidden_out[...] = hidden.astype(BF)
        slope_out[...] = pullback(jnp.ones_like(preact))[0]

    return local_call(
        kernel,
        [((2 * hid, rows), BF), ((2 * hid, rows), F32), ((2 * hid, width), BF), ((din, rows), BF)],
        [pltpu.VMEM((2 * hid, din), BF)],
        flops=4 * hid * rows * din, moved=4 * rows * din,
        operands=(own, other, *embs), room=ROOM["again"],
    )


def head_grads(phis, hidden, slope, second, emb):
    _, width = phis[0].shape
    din, rows = emb.shape
    hid = hidden.shape[0] // 2

    def kernel(p0, p1, p2, p3, hid_ref, slope_ref, w_ref, emb_ref, first_out, second_out, bias_out, sent, phi):
        join((p0, p1, p2, p3), phi)
        grad = nt_dot(w_ref[...], phi[...]) * slope_ref[...]
        low = grad.astype(BF)
        rest = (grad - low.astype(F32)).astype(BF)
        ones = jnp.ones((16, rows), BF)
        firsts = nt_dot(low, emb_ref[...])
        seconds = jnp.dot(hid_ref[...], phi[...], preferred_element_type=F32)
        first_out[...] = firsts[:hid]
        second_out[...] = seconds[:hid]
        bias_out[...] = nt_dot(ones, low[:hid]) + nt_dot(ones, rest[:hid])
        sent[:hid, :din] = firsts[hid:].astype(BF)
        sent[:hid, din:] = seconds[hid:].astype(BF)
        sent[hid:, :] = jnp.zeros((16, din + width), BF)
        sent[hid:, :hid] = (nt_dot(ones, low[hid:]) + nt_dot(ones, rest[hid:])).astype(BF)

    return local_call(
        kernel,
        [((hid, din), F32), ((hid, width), F32), ((16, hid), F32), ((hid + 16, din + width), BF)],
        [pltpu.VMEM((rows, width), BF)],
        flops=4 * hid * rows * (din + 2 * width), moved=4 * rows * din,
        operands=(*phis, hidden, slope, second, emb), room=ROOM["bwd"],
    )


def head_join(first, second, bias, got):
    hid, din = first.shape

    def kernel(first_ref, second_ref, bias_ref, got_ref, first_out, second_out, bias_out):
        first_out[...] = first_ref[...] + got_ref[:hid, :din].astype(F32)
        second_out[...] = second_ref[...] + got_ref[:hid, din:].astype(F32)
        bias_out[...] = bias_ref[:1, :] + got_ref[hid:, :hid][:1, :].astype(F32)

    return local_call(
        kernel, [(first.shape, F32), (second.shape, F32), ((1, hid), F32)],
        moved=12 * hid * din, operands=(first, second, bias, got), room=ROOM["join"], keep=False,
    )


def make_body(count, groups):
    deep = count // Z
    levels = deep.bit_length() - 1

    def send(value, pairs):
        return lax.ppermute(value, "center", pairs)

    def swap(value, bit):
        return send(value, [(i, i ^ bit) for i in range(count)])

    def owner(i):
        block = (i & 1) * 4 + ((i >> 1) & 3)
        return deep * block + i // Z

    def inner_body(embeddings, first_weight, first_bias, second_weight, centers, coefficients, cotangent):
        feat_width = centers.shape[1]
        factor = 16.0 / feat_width
        rows = embeddings.shape[0]
        blk = rows // 8
        _, hid = first_weight.shape
        place = lax.axis_index("center")
        spot = place[None]
        xbit, ybit = (place >> 1) & 1, (place >> 2) & 1
        plane = [xbit, ybit]

        local = embeddings.T
        slabs = [
            jnp.concatenate([local[:, (4 * c + p) * blk:][:, :blk] for c in range(2)], axis=1)
            for p in range(4)
        ]
        slabs = arrange(slabs, plane)
        got = {k: swap(slabs[k], k * X) for k in (3, 1, 2)}
        block = jnp.concatenate([slabs[0], got[1], got[2], got[3]], axis=0)

        high = first_bias.astype(BF)
        low = (first_bias - high.astype(F32)).astype(BF)
        spread = jnp.concatenate([high, low])
        hids = lax.broadcasted_iota(jnp.int32, (hid, 2 * hid), 0)
        slots = lax.broadcasted_iota(jnp.int32, (hid, 2 * hid), 1) % hid
        bias_cols = jnp.where(hids == slots, spread[None, :], jnp.zeros((), BF))
        bias_cols = jnp.pad(bias_cols, ((0, 0), (0, -2 * hid % 128)))
        own_weights = jnp.concatenate([first_weight.T, second_weight, bias_cols], axis=1)
        got = {k: swap(own_weights, k * X) for k in (3, 1, 2)}
        weights = [own_weights, got[1], got[2], got[3]]
        core_weights = swap(own_weights, CORE)

        blocks = [block] + [swap(block, k * Z) for k in range(1, deep)]
        late = deep // 2
        order = [[k for k in range(deep) if k != late], [late]] if deep > 1 else [[0]]
        others = [swap(jnp.concatenate([blocks[k] for k in levels_of], axis=0), CORE) for levels_of in order]
        mine, theirs, emb_own = head_pass(spot, weights, blocks, others, order, feat_width, count)
        total = mine + swap(theirs, CORE)

        def deep_sum(value):
            for k in range(levels):
                low_value = value.astype(BF)
                value = low_value.astype(F32) + swap(low_value, Z << k).astype(F32)
            return value

        feature_sum = deep_sum(total)
        squashed = jnp.tanh(feature_sum)
        own_feats = squashed.astype(BF)
        got = {k: swap(own_feats, k * X) for k in (3, 1, 2)}

        cot, cot_rows = cot_pass(spot, cotangent.T)

        emb_x, emb_y = swap(emb_own, X), swap(emb_own, Y)
        emb_xy = swap(emb_y, X)

        coef_own = coefficients.T
        sets = [
            (centers, coef_own),
            (swap(centers, CORE), swap(coef_own, CORE)),
        ]
        norms = []
        for points, coef in sets:
            wide = points.astype(F32)
            norms.append(jnp.sum(wide * wide, axis=1)[None, :])
        slopes = slope_pass(cot_rows, (sets[0][1], sets[1][1]))
        feats = [own_feats, got[1], got[2], got[3]]
        *near_out, grad0, grad1 = point_pass(feats[:2], slopes[:2], sets, norms, factor, (F32, BF))
        *far_out, grad2, grad3 = point_pass(feats[2:], slopes[2:], sets, norms, factor, (BF, BF))
        grads = [grad0, grad1, grad2, grad3]
        kern0, kern1, low0, low1, col0, col1 = zip(near_out, far_out)

        def plane_sum(parts):
            got = [swap(parts[k], k * X) for k in (3, 1, 2)]
            return parts[0].astype(F32) + sum(part.astype(F32) for part in got)

        feature_grad = deep_sum(plane_sum(grads))
        phi_own = (feature_grad * (1.0 - squashed * squashed)).astype(BF)
        got = {k: swap(phi_own, k * X) for k in (3, 1, 2)}
        phis = [phi_own, got[1], got[2], got[3]]

        far_cen, far_coef, *preds = far_points(
            feats, cot, (kern0, kern1), low1, col1, sets[1][0], (sets[0][1], sets[1][1]), factor
        )
        got = {k: swap(preds[k], k * X) for k in (3, 1, 2)}
        parts = [preds[0], got[1], got[2], got[3]]
        for k in reversed(range(levels)):
            keep, sent = pred_step(spot, parts, k)
            parts = [keep, swap(sent, Z << k)]
        preds = sum(part.astype(F32) for part in parts)
        predictions = send(preds.astype(BF), [(i, owner(i)) for i in range(count)]).astype(F32)

        got_cen, got_coef = swap(far_cen, CORE), swap(far_coef, CORE)
        center_grad, coef_grad = near_points(
            feats, cot, kern0, low0, col0, centers, got_cen, got_coef, factor
        )
        coef_grad = coef_grad.T

        hidden, slope, second, emb_rows = head_again(
            own_weights, core_weights, [emb_own, emb_x, emb_y, emb_xy], feat_width
        )
        first_grad, second_grad, bias_grad, sent = head_grads(phis, hidden, slope, second, emb_rows)
        got = swap(sent, CORE)
        first_grad, second_grad, bias_grad = head_join(first_grad, second_grad, bias_grad, got)
        first_grad = first_grad.T
        bias_grad = bias_grad[0]
        if groups > 1:
            first_grad, second_grad, center_grad = (
                lax.psum_scatter(first_grad.astype(BF), "dp", scatter_dimension=0, tiled=True).astype(F32),
                lax.psum_scatter(second_grad.astype(BF), "dp", scatter_dimension=1, tiled=True).astype(F32),
                lax.psum_scatter(center_grad.astype(BF), "dp", scatter_dimension=1, tiled=True).astype(F32),
            )
            bias_grad, coef_grad = (
                lax.psum(bias_grad.astype(BF), "dp").astype(F32),
                lax.psum(coef_grad.astype(BF), "dp").astype(F32),
            )
        return (predictions, first_grad, bias_grad, second_grad, center_grad, coef_grad)

    return inner_body


def solution(mesh):
    placed = (
        P("dp", "center"),
        P(None, "center"),
        P("center"),
        P("center", None),
        P("center", None),
        P("center", None),
        P("dp", None),
    )
    count, groups = mesh.shape["center"], mesh.shape["dp"]
    return jax.shard_map(
        make_body(count, groups),
        mesh=mesh,
        in_specs=placed,
        out_specs=(
            P(("dp", "center"), None),
            P("dp", "center"),
            P("center"),
            P("center", "dp"),
            P("center", "dp"),
            P("center", None),
        ),
        check_vma=False,
    )
```
